32 devices in a mesh: groups: 2 (over y), ha: 4 (over z), wa: 2 (over x), ta: 2 (over core).
Axes of the slice: x: 2, y: 2, z: 4, core: 2. Of those that a mesh axis runs over, the one named last changes fastest.
Arguments:
- tokens: bfloat16 [4, 1024, 3072], P(('groups', 'ta'), ('ha', 'wa')), parts along dimension 0, may hold values from -400 to 400
- mod_scale: float32 [6144], P('groups'), parts along dimension 0, may hold values from -3 to 3
- mod_shift: float32 [6144], P('groups'), parts along dimension 0, may hold values from -3 to 3
- proj_weight: bfloat16 [3072, 64], replicated, may hold values from -0.109375 to 0.109375
- proj_bias: float32 [64], replicated, may hold values from -3 to 3
- conv_weight: bfloat16 [3, 3, 16, 512], replicated, may hold values from -0.5 to 0.5
- conv_bias: float32 [512], replicated, may hold values from -3 to 3
- up_weight: bfloat16 [4, 4, 512, 256], P(None, None, 'ha', 'wa'), may hold values from -0.125 to 0.125
- up_bias: float32 [256], replicated, may hold values from -3 to 3
- out_weight: bfloat16 [3, 3, 256, 256], replicated, may hold values from -0.125 to 0.125
- out_bias: float32 [256], replicated, may hold values from -3 to 3
Outputs:
- decoded: bfloat16 [32, 32, 64, 256], P(('groups', 'ta'), 'ha', 'wa'), parts along dimension 0
The draws below stay inside these ranges and needn't reach their ends.
There are 2 independent parts, one for each index of `groups`. The reference program is written for one: setup_inputs(seed, part) draws one part's arguments, and reference() takes and returns one part's arrays. A program takes and returns all parts, laid end to end along the dimension named above; an argument that names none is the same for every part. Nothing has to cross between parts.
All inputs are finite; a program needn't handle non-finite values.
Results may differ from the reference program's by a relative error of at most 0.0057.
Values may be sent and summed in bfloat16 or wider, within the bound.
No kernel may reach another device: no remote copies, remote signals or barrier semaphores. Data moves between devices by JAX's collectives and lax.ppermute only.
A program may use at most 64 MiB of HBM per device.

```python
import math
import jax
import jax.numpy as jnp
from jax import lax

D = 3072
C_LAT = 16
C_IN = 512
C_UP = 256
TH = 2
TW = 8
F_DEV = 8
BLOCKS = 2
TILE_COLS = 2
SEQ_BLOCK = 1024
FRAMES = 16
H_TOK = 8
W_TOK = 16
N_HA = 4


def draw_tokens(key, part):
    key_noise, key_feature, key_token = jax.random.split(key, 3)
    shape_all = (BLOCKS, SEQ_BLOCK, D)
    feature_scale = jnp.exp(jax.random.uniform(key_feature, (D,), jnp.float32, 0.0, math.log(10.0)))
    token_scale = jnp.exp(jax.random.uniform(key_token, (BLOCKS, SEQ_BLOCK, 1), jnp.float32, 0.0, math.log(10.0)))
    noise_part = jnp.clip(jax.random.normal(key_noise, shape_all, jnp.float32), -4.0, 4.0)
    values = token_scale * feature_scale * noise_part
    return jnp.clip(values, -400.0, 400.0).astype(jnp.bfloat16)


def shard_levels(key, extent, shards, least, largest):
    gain = 1.0
    for dim, shards_of in shards:
        heights = jax.random.uniform(jax.random.fold_in(jax.random.fold_in(key, 6), dim), (shards_of,), jnp.float32, least / len(shards), largest / len(shards))
        gain = gain * jnp.repeat(jnp.exp(heights), extent[dim] // shards_of).reshape((-1,) + (1,) * (len(extent) - 1 - dim))
    return gain


def gaussian(rng, dims, width, reach, cuts=(), dtype=jnp.bfloat16):
    entries = jax.random.normal(rng, dims, jnp.float32) * width
    if len(cuts) > 0:
        entries = shard_levels(rng, dims, cuts, -0.22, 0.18) * entries
    return jnp.clip(entries, min=-reach, max=reach).astype(dtype)


def setup_inputs(seed: int = 0, part: int = 0) -> dict:
    key_of = jax.random.split(jax.random.key(seed), 12)
    part_splits = jax.random.split(jax.random.fold_in(key_of[11], part), 12)
    tokens = draw_tokens(jax.random.fold_in(jax.random.fold_in(key_of[11], part), 71), part)
    mod_scale = gaussian(part_splits[1], (D,), 0.5, 3.0, (), jnp.float32)
    mod_shift = gaussian(part_splits[2], (D,), 0.5, 3.0, (), jnp.float32)
    proj_weight = gaussian(key_of[3], (D, 4 * C_LAT), D ** -0.5, 0.109375)
    proj_bias = gaussian(key_of[4], (4 * C_LAT,), 0.5, 3.0, (), jnp.float32)
    conv_weight = gaussian(key_of[5], (3, 3, C_LAT, C_IN), (9 * C_LAT) ** -0.5, 0.5)
    conv_bias = gaussian(key_of[6], (C_IN,), 0.5, 3.0, (), jnp.float32)
    up_weight = gaussian(key_of[7], (4, 4, C_IN, C_UP), (4 * C_IN) ** -0.5, 0.125, ((2, 4), (3, 2)))
    up_bias = gaussian(key_of[8], (C_UP,), 0.5, 3.0, (), jnp.float32)
    out_weight = gaussian(key_of[9], (3, 3, C_UP, C_UP), (9 * C_UP) ** -0.5, 0.125)
    out_bias = gaussian(key_of[10], (C_UP,), 0.5, 3.0, (), jnp.float32)
    return dict(tokens=tokens, mod_scale=mod_scale, mod_shift=mod_shift, proj_weight=proj_weight, proj_bias=proj_bias, conv_weight=conv_weight, conv_bias=conv_bias, up_weight=up_weight, up_bias=up_bias, out_weight=out_weight, out_bias=out_bias)


def final_layer(tokens, mod_scale, mod_shift, proj_weight, proj_bias):
    values = tokens.astype(jnp.float32)
    center = values - lax.optimization_barrier(jnp.mean(values, axis=-1, keepdims=True))
    spread = lax.optimization_barrier(jnp.mean(center * center, axis=-1, keepdims=True))
    normed = center * lax.rsqrt(spread + 1e-06) * (1.0 + mod_scale) + mod_shift
    normed = normed.astype(jnp.bfloat16)
    patch = jnp.dot(normed, proj_weight, preferred_element_type=jnp.float32) + proj_bias
    return patch.astype(jnp.bfloat16)

def conv_three(padded, weight):
    height = padded.shape[1] - 2
    breadth = padded.shape[2] - 2
    summed = None
    for offset_row in range(3):
        for offset_col in range(3):
            window = padded[:, offset_row:offset_row + height, offset_col:offset_col + breadth, :]
            product = jnp.dot(window, weight[offset_row, offset_col], preferred_element_type=jnp.float32)
            summed = product if summed is None else summed + product
    return summed

def spread_taps(padded, weight):
    height = padded.shape[1] - 1
    breadth = padded.shape[2] - 1
    parity_rows = []
    for row_parity in range(2):
        parity_cols = []
        for col_parity in range(2):
            summed = None
            for row_shift, row_tap in ((1, row_parity), (0, row_parity + 2)):
                for col_shift, col_tap in ((1, col_parity), (0, col_parity + 2)):
                    window = padded[:, row_shift:row_shift + height, col_shift:col_shift + breadth, :]
                    product = jnp.dot(window, weight[row_tap, col_tap], preferred_element_type=jnp.float32)
                    summed = product if summed is None else summed + product
            parity_cols.append(summed)
        parity_rows.append(jnp.stack(parity_cols, axis=3))
    stacked = jnp.stack(parity_rows, axis=2)
    return stacked.reshape(stacked.shape[0], 2 * height, 2 * breadth, stacked.shape[-1])

def pad_frame(values):
    return jnp.pad(values, ((0, 0), (1, 1), (1, 1), (0, 0)))

def reference(tokens, mod_scale, mod_shift, proj_weight, proj_bias, conv_weight, conv_bias, up_weight, up_bias, out_weight, out_bias):
    flat = tokens.reshape(BLOCKS * SEQ_BLOCK, D)
    patch = final_layer(flat, mod_scale, mod_shift, proj_weight, proj_bias)
    arranged = patch.reshape(BLOCKS, F_DEV, TH, TW, N_HA, TILE_COLS, C_LAT, 2, 2)
    arranged = arranged.transpose(0, 1, 4, 2, 7, 5, 3, 8, 6)
    latent = arranged.reshape(FRAMES, 2 * H_TOK, 2 * W_TOK, C_LAT)

    def decode_frame(latent_frame):
        features = jax.nn.silu(conv_three(pad_frame(latent_frame[None]), conv_weight) + conv_bias)
        features = features.astype(jnp.bfloat16)
        extended = spread_taps(pad_frame(features), up_weight)
        upsampled = jax.nn.silu(extended[:, 1:-1, 1:-1, :] + up_bias).astype(jnp.bfloat16)
        result = conv_three(pad_frame(upsampled), out_weight) + out_bias
        return result.astype(jnp.bfloat16)[0]
    return lax.map(decode_frame, latent)
```

```python
import functools

import jax
import jax.numpy as jnp
from jax import lax
from jax.experimental import pallas as pl
from jax.experimental.pallas import tpu as pltpu
from jax.sharding import PartitionSpec as P

C_LAT = 16
TH = 2
TW = 8
LANES = 128


def swap(count):
    return [(i, i ^ 1) for i in range(count)]


def inner_swap(count):
    pairs = [(i, i + 1) for i in range(1, count - 1, 2)]
    return pairs + [(j, i) for i, j in pairs]


def silu(value):
    return value * jax.nn.sigmoid(value)


def padded_2(cells, sides, width):
    for axis, dim in sides:
        count = lax.axis_size(axis)
        ends = count - 1
        head = lax.slice_in_dim(cells, 0, width, axis=dim)
        tail = lax.slice_in_dim(cells, cells.shape[dim] - width, cells.shape[dim], axis=dim)
        cells = jnp.concatenate(
            [
                lax.ppermute(tail, axis, [(i, (i + 1) % count) for i in range(ends)]),
                cells,
                lax.ppermute(head, axis, [((i + 1) % count, i) for i in range(ends)]),
            ],
            axis=dim,
        )
    return cells


def final_layer(tokens, mod_scale, mod_shift, proj_weight, proj_bias):
    values = tokens.astype(jnp.float32)
    center = values - jnp.mean(values, axis=-1, keepdims=True)
    spread = jnp.mean(center * center, axis=-1, keepdims=True)
    normed = center * lax.rsqrt(spread + 1e-06) * (1.0 + mod_scale) + mod_shift
    normed = normed.astype(jnp.bfloat16)
    patch = jnp.dot(normed, proj_weight, preferred_element_type=jnp.float32) + proj_bias
    return patch.astype(jnp.bfloat16)


def cells_first(values):
    shape = values.shape[:-1]
    return values.reshape(shape + (C_LAT, 4)).swapaxes(-1, -2).reshape(shape + (4 * C_LAT,))


def token_grid(patch, rows, cols):
    tiles = rows * cols
    count, lanes = patch.shape
    each = count // tiles
    if each % (TH * TW) == 0:
        frames = each // (TH * TW)
        grid = patch.reshape(frames, TH, TW, rows, cols, lanes).transpose(3, 1, 4, 2, 0, 5)
        grid = grid.reshape(rows * TH, cols * TW, frames, lanes)
        grid = jnp.pad(grid, ((1, 1), (1, 1), (0, 0), (0, 0)))
        sent = jnp.stack(
            [
                grid[h * TH : (h + 1) * TH + 2, w * TW : (w + 1) * TW + 2]
                for h in range(rows)
                for w in range(cols)
            ]
        )
        arrived = lax.all_to_all(
            sent.reshape(tiles, (TH + 2) * (TW + 2) * frames, lanes),
            ("ha", "wa"),
            split_axis=0,
            concat_axis=0,
            tiled=True,
        )
        arrived = arrived.reshape(tiles, TH + 2, TW + 2, frames, lanes).transpose(1, 2, 0, 3, 4)
        return arrived.reshape(TH + 2, TW + 2, tiles * frames, lanes)
    arrived = lax.all_to_all(
        patch.reshape(each, tiles, lanes), ("ha", "wa"), split_axis=1, concat_axis=0, tiled=True
    )
    grid = arrived.reshape(count // (TH * TW), TH, TW, lanes)
    grid = padded_2(grid, (("ha", 1), ("wa", 2)), 1)
    return grid.transpose(1, 2, 0, 3)


def gathered_pieces(weight, rows):
    core = lax.axis_index("ta")
    place = lax.axis_index("ha")
    taps = weight.shape[0] // 2
    own = lax.dynamic_slice_in_dim(weight, core * taps, taps, 0)
    across = swap(2)
    outer, inner = swap(rows), inner_swap(rows)
    by_outer, by_inner = [], []
    last_outer, last_inner = own, own
    for step in range(rows - 1):
        new_outer = lax.ppermute(last_inner, "ha", outer)
        by_outer.append(new_outer)
        if step < rows - 2:
            new_inner = lax.ppermute(last_outer, "ha", inner)
            by_inner.append(new_inner)
            last_inner = new_inner
        last_outer = new_outer
    pieces = [own]
    for k in range(1, rows):
        chosen = by_outer[k - 1]
        for i in range(rows):
            count = outer_count(i, rows)
            if k > count:
                chosen = jnp.where(place == i, by_inner[k - count - 1], chosen)
        pieces.append(chosen)
    others = [lax.ppermute(piece, "wa", across) for piece in pieces]
    mine = pieces[1:] + others
    return mine, [lax.ppermute(piece, "ta", across) for piece in mine]


def outer_count(i, rows):
    return rows - 1 - i if i % 2 == 0 else i


def arrival_order(rows):
    table = []
    for i in range(rows):
        count = outer_count(i, rows)
        sign = 1 if i % 2 == 0 else -1
        order = [i] + [i + sign * t for t in range(1, count + 1)]
        order += [i - sign * t for t in range(1, rows - count)]
        table.append(order)
    return table


def tile_kernel(units_k, units_n, place_ref, tok_ref, cw_ref, cb_ref, ub_ref, ow_ref, ob_ref, *rest):
    n_pieces = units_k * units_n - 1
    w_ref = rest[0]
    mine = rest[1 : 1 + n_pieces]
    theirs = rest[1 + n_pieces : 1 + 2 * n_pieces]
    o_ref, wide, feat, cols, even, odd, tall = rest[1 + 2 * n_pieces :]
    rows_blk = tok_ref.shape[0] - 1
    cols_blk = tok_ref.shape[1] - 1
    frames = tok_ref.shape[2]
    lanes = tok_ref.shape[3]
    c_lat = cw_ref.shape[1]
    c_in = cw_ref.shape[2]
    c_up = ob_ref.shape[1]
    has_up = place_ref[0] > 0
    has_down = place_ref[1] > 0
    has_left = place_ref[2] > 0
    has_right = place_ref[3] > 0
    core = place_ref[4]
    column = place_ref[5]
    wide[...] = jnp.zeros_like(wide)
    for p in range(2):
        for q in range(2):
            for r in range(3):
                for s in range(3):
                    tr, a = divmod(p + r, 2)
                    tc, e = divmod(q + s, 2)
                    base = (tr * 2 + tc) * lanes + (a * 2 + e) * c_lat
                    at = (p * 2 + q) * c_in
                    wide[base : base + c_lat, at : at + c_in] = cw_ref[r * 3 + s]
    tok = tok_ref[...].astype(jnp.float32)
    block = jnp.concatenate(
        [tok[tr : tr + rows_blk, tc : tc + cols_blk] for tr in range(2) for tc in range(2)], axis=-1
    )
    block = block.reshape(rows_blk * cols_blk * frames, 4 * lanes).astype(jnp.bfloat16)
    for p in range(2):
        for q in range(2):
            at = (p * 2 + q) * c_in
            value = jnp.dot(block, wide[:, at : at + c_in], preferred_element_type=jnp.float32)
            value = silu(value + cb_ref[...]).astype(jnp.bfloat16).astype(jnp.float32)
            value = value.reshape(rows_blk, cols_blk, frames, c_in)
            for m in range(rows_blk):
                for n in range(cols_blk):
                    piece = value[m, n]
                    if m == 0 and p == 0:
                        piece = jnp.where(has_up, piece, 0.0)
                    if m == rows_blk - 1 and p == 1:
                        piece = jnp.where(has_down, piece, 0.0)
                    if n == 0 and q == 0:
                        piece = jnp.where(has_left, piece, 0.0)
                    if n == cols_blk - 1 and q == 1:
                        piece = jnp.where(has_right, piece, 0.0)
                    feat[2 * m + p, 2 * n + q] = piece
    height = 2 * rows_blk - 1
    breadth = 2 * cols_blk - 1
    rows_pad = cols.shape[0] // height
    filled = breadth * frames
    ck = c_in // units_k
    cn = c_up // units_n
    for half in range(2):
        shift = 1 - core if half == 0 else core
        for r in range(height):
            for cs in range(2):
                value = feat[r + shift, cs : cs + breadth].reshape(filled, c_in).astype(jnp.bfloat16)
                for k in range(units_k):
                    at = ((half * units_k + k) * 2 + cs) * ck
                    cols[r * rows_pad : r * rows_pad + filled, at : at + ck] = value[:, k * ck : (k + 1) * ck]

    def tap(half, k, j, a, v):
        if k == 0 and j == 0:
            side = core if half == 0 else 1 - core
            return w_ref[2 * side + a, v]
        at = k - 1 if j == 0 else units_k - 1 + (j - 1) * units_k + k
        return (mine if half == 0 else theirs)[at][a, v]

    for j in range(units_n):
        to = pl.multiple_of((column if j == 0 else 1 - column) * cn, cn)
        bias = ub_ref[:, pl.ds(to, cn)]
        for a in range(2):
            stacked = jnp.concatenate(
                [
                    jnp.concatenate([tap(half, k, j, a, 2 * (1 - cs) + b) for b in range(2)], axis=1)
                    for half in range(2)
                    for k in range(units_k)
                    for cs in range(2)
                ],
                axis=0,
            )
            total = jnp.dot(cols[...], stacked, preferred_element_type=jnp.float32)
            pair = []
            for b in range(2):
                value = silu(total[:, b * cn : (b + 1) * cn] + bias)
                value = value.reshape(height, rows_pad, cn)[:, :filled]
                pair.append(value.reshape(height, breadth, frames, cn))
            for r in range(height):
                line = 2 * r + a
                v0, v1 = pair[0][r], pair[1][r]
                v0 = jnp.concatenate([jnp.where(has_left, v0[:1], 0.0), v0[1:]], axis=0)
                v1 = jnp.concatenate([v1[:-1], jnp.where(has_right, v1[-1:], 0.0)], axis=0)
                if line == 0:
                    v0, v1 = jnp.where(has_up, v0, 0.0), jnp.where(has_up, v1, 0.0)
                if line == 2 * height - 1:
                    v0, v1 = jnp.where(has_down, v0, 0.0), jnp.where(has_down, v1, 0.0)
                ev = jnp.stack([v0, v1], axis=1).reshape(2 * filled, cn)
                od = jnp.stack([v1[:-1], v0[1:]], axis=1).reshape(2 * (filled - frames), cn)
                even[line, :, pl.ds(to, cn)] = ev.astype(jnp.bfloat16)
                odd[line, :, pl.ds(to, cn)] = od.astype(jnp.bfloat16)
    out_h, out_w = o_ref.shape[1], o_ref.shape[2]
    span = out_w * frames
    step = 2
    for y in range(0, out_h, step):
        total = None
        for r in range(3):
            for s in range(3):
                if s == 1:
                    lhs = odd[y + r : y + r + step]
                else:
                    lhs = even[y + r : y + r + step, s * frames : s * frames + span]
                product = jnp.dot(
                    lhs.reshape(step * span, c_up), ow_ref[r * 3 + s], preferred_element_type=jnp.float32
                )
                total = product if total is None else total + product
        total = total + ob_ref[...]
        part = tall.shape[2]
        for h in range(tall.shape[0]):
            tall[h] = total[:, h * part : (h + 1) * part]
            for d in range(step):
                for f in range(frames):
                    line = tall[h, pl.ds(d * span + f, out_w, stride=frames), :]
                    o_ref[f, y + d, :, h * part : (h + 1) * part] = line.astype(jnp.bfloat16)


def tile_call(place, tok, cw, cb, ub, ow, ob, weights, units_k, units_n):
    rows_blk, cols_blk, frames, lanes = tok.shape[0] - 1, tok.shape[1] - 1, tok.shape[2], tok.shape[3]
    c_in, c_up = cw.shape[2], ob.shape[1]
    height, breadth = 2 * rows_blk - 1, 2 * cols_blk - 1
    rows_pad = -(-breadth * frames // 16) * 16
    out_shape = (frames, 2 * height - 2, 2 * breadth - 2, c_up)
    vmem = pl.BlockSpec(memory_space=pltpu.VMEM)
    return pl.pallas_call(
        functools.partial(tile_kernel, units_k, units_n),
        out_shape=jax.ShapeDtypeStruct(out_shape, jnp.bfloat16),
        in_specs=[pl.BlockSpec(memory_space=pltpu.SMEM)] + [vmem] * (6 + len(weights)),
        out_specs=vmem,
        scratch_shapes=[
            pltpu.VMEM((4 * lanes, 4 * c_in), jnp.bfloat16),
            pltpu.VMEM((2 * rows_blk, 2 * cols_blk, frames, c_in), jnp.float32),
            pltpu.VMEM((height * rows_pad, 4 * c_in), jnp.bfloat16),
            pltpu.VMEM((2 * height, 2 * breadth * frames, c_up), jnp.bfloat16),
            pltpu.VMEM((2 * height, 2 * (breadth - 1) * frames, c_up), jnp.bfloat16),
            pltpu.VMEM((c_up // LANES, 2 * out_shape[2] * frames, LANES), jnp.float32),
        ],
        compiler_params=pltpu.CompilerParams(vmem_limit_bytes=48 << 20),
        name="tile",
    )(place, tok, cw, cb, ub, ow, ob, *weights)


def per_device(
    tokens,
    mod_scale,
    mod_shift,
    proj_weight,
    proj_bias,
    conv_weight,
    conv_bias,
    up_weight,
    up_bias,
    out_weight,
    out_bias,
):
    count_rows = lax.axis_size("ha")
    count_cols = lax.axis_size("wa")
    row_place = lax.axis_index("ha")
    col_place = lax.axis_index("wa")
    ck, cn = up_weight.shape[2], up_weight.shape[3]
    c_in, c_up = conv_weight.shape[3], out_weight.shape[3]
    conv_flat = conv_weight.reshape(9, C_LAT, c_in)
    split = (
        count_cols == 2
        and lax.axis_size("ta") == 2
        and count_rows % 2 == 0
        and ck % LANES == 0
        and cn % LANES == 0
    )
    if split:
        order = jnp.asarray(arrival_order(count_rows), jnp.int32)[row_place]
        mine, theirs = gathered_pieces(up_weight, count_rows)
        weights = [up_weight] + mine + theirs
        units_k, units_n = count_rows, count_cols
        conv_flat = jnp.concatenate(
            [lax.dynamic_slice_in_dim(conv_flat, order[k] * ck, ck, 2) for k in range(count_rows)], axis=2
        )
        conv_bias = jnp.concatenate(
            [lax.dynamic_slice_in_dim(conv_bias, order[k] * ck, ck, 0) for k in range(count_rows)]
        )
    else:
        whole = lax.all_gather(up_weight, "wa", axis=3, tiled=True)
        whole = lax.all_gather(whole, "ha", axis=2, tiled=True)
        weights = [whole]
        units_k, units_n = 1, 1
    local_tokens = tokens.reshape(tokens.shape[1], tokens.shape[2])
    patch = final_layer(
        local_tokens, mod_scale, mod_shift, cells_first(proj_weight), cells_first(proj_bias)
    )
    tok = token_grid(patch, count_rows, count_cols)
    place = jnp.stack(
        [
            row_place > 0,
            row_place < count_rows - 1,
            col_place > 0,
            col_place < count_cols - 1,
            lax.axis_index("ta") if split else 0 * row_place,
            col_place if split else 0 * row_place,
        ]
    ).astype(jnp.int32)
    return tile_call(
        place,
        tok,
        conv_flat,
        conv_bias[None],
        up_bias[None],
        out_weight.reshape(9, c_up, c_up),
        out_bias[None],
        weights,
        units_k,
        units_n,
    )


def solution(mesh):
    placed = (
        P(("groups", "ta"), ("ha", "wa"), None),
        P("groups"),
        P("groups"),
        P(),
        P(),
        P(),
        P(),
        P(None, None, "ha", "wa"),
        P(),
        P(),
        P(),
    )
    return jax.shard_map(
        per_device,
        mesh=mesh,
        in_specs=placed,
        out_specs=P(("groups", "ta"), "ha", "wa", None),
        check_vma=False,
    )
```

```python
import functools

import jax
import jax.numpy as jnp
from jax import lax
from jax.experimental import pallas as pl
from jax.experimental.pallas import tpu as pltpu
from jax.sharding import PartitionSpec as P


C_LAT = 16
TH = 2
TW = 8
LANES = 128
VMEM_BYTES = 10 << 20
UNITS = 4
VMEM = pl.BlockSpec(memory_space=pltpu.VMEM)
ANYWHERE = pl.BlockSpec(memory_space=pl.ANY)


def silu(value):
    return value * jax.nn.sigmoid(value)


def padded_2(cells, sides, width):
    for axis, dim in sides:
        count = lax.axis_size(axis)
        ends = count - 1
        head = lax.slice_in_dim(cells, 0, width, axis=dim)
        tail = lax.slice_in_dim(cells, cells.shape[dim] - width, cells.shape[dim], axis=dim)
        cells = jnp.concatenate(
            [
                lax.ppermute(tail, axis, [(i, (i + 1) % count) for i in range(ends)]),
                cells,
                lax.ppermute(head, axis, [((i + 1) % count, i) for i in range(ends)]),
            ],
            axis=dim,
        )
    return cells


def kept(value):
    return pltpu.with_memory_space_constraint(value, pltpu.HBM)


def brought(sources, targets, sems):
    copies = [
        pltpu.make_async_copy(source, target, sems.at[i])
        for i, (source, target) in enumerate(zip(sources, targets))
    ]
    for copy in copies:
        copy.start()
    return copies


def front_kernel(rows, cols, *refs):
    sources, o_ref = refs[:5], refs[5]
    tok_ref, scale_ref, shift_ref, pw_ref, pb_ref, sems, patch = refs[6:13]
    copies = brought(sources, refs[6:11], sems)
    count, lanes = patch.shape
    width = pw_ref.shape[0]
    copies[0].wait()
    values = tok_ref[...].astype(jnp.float32)
    center = values - jnp.mean(values, axis=-1, keepdims=True)
    spread = jnp.mean(center * center, axis=-1, keepdims=True)
    for copy in copies[1:]:
        copy.wait()
    normed = center * lax.rsqrt(spread + 1e-06) * (1.0 + scale_ref[...]) + shift_ref[...]
    value = lax.dot_general(
        normed.astype(jnp.bfloat16),
        pw_ref[...],
        (((1,), (1,)), ((), ())),
        preferred_element_type=jnp.float32,
    )
    value = (value + pb_ref[...]).astype(jnp.bfloat16)
    source = lax.broadcasted_iota(jnp.int32, (width, lanes), 0)
    place = lax.broadcasted_iota(jnp.int32, (width, lanes), 1)
    chosen = source == (place % C_LAT) * (width // C_LAT) + place // C_LAT
    chosen = jnp.where(chosen & (place < width), 1.0, 0.0).astype(jnp.bfloat16)
    patch[...] = jnp.dot(value, chosen, preferred_element_type=jnp.float32)
    if len(refs) == 13:
        o_ref[...] = patch[...].astype(jnp.bfloat16)
        return
    window = refs[13]
    tiles = rows * cols
    frames = count // (tiles * TH * TW)
    window[...] = jnp.zeros_like(window)
    for h in range(rows):
        for w in range(cols):
            for f in range(frames):
                for d in range(TH + 2):
                    row = h * TH + d - 1
                    if not 0 <= row < rows * TH:
                        continue
                    base = (f * TH + row % TH) * TW * tiles + (row // TH) * cols
                    to = (((h * cols + w) * frames + f) * (TH + 2) + d) * (TW + 2)
                    window[to + 1 : to + 1 + TW, :] = patch[pl.ds(base + w, TW, stride=tiles), :]
                    if w > 0:
                        at = base + (TW - 1) * tiles + w - 1
                        window[to : to + 1, :] = patch[at : at + 1, :]
                    if w < cols - 1:
                        at = base + w + 1
                        window[to + 1 + TW : to + 2 + TW, :] = patch[at : at + 1, :]
    o_ref[...] = window[...].reshape(o_ref.shape).astype(jnp.bfloat16)


def token_windows(tokens, mod_scale, mod_shift, proj_weight, proj_bias, rows, cols):
    tiles = rows * cols
    count = tokens.shape[0]
    around = (TH + 2) * (TW + 2)
    vmem, anyw = VMEM, ANYWHERE
    args = (tokens, mod_scale[None], mod_shift[None], proj_weight.T, proj_bias[None])
    scratch = [pltpu.VMEM(arg.shape, arg.dtype) for arg in args]
    scratch += [pltpu.SemaphoreType.DMA((len(args),)), pltpu.VMEM((count, LANES), jnp.float32)]
    params = pltpu.CompilerParams(vmem_limit_bytes=VMEM_BYTES)
    each = count // tiles
    if each % (TH * TW) == 0:
        frames = each // (TH * TW)
        sent = pl.pallas_call(
            functools.partial(front_kernel, rows, cols),
            out_shape=jax.ShapeDtypeStruct((tiles, frames * around, LANES), jnp.bfloat16),
            in_specs=[anyw] * 5,
            out_specs=vmem,
            scratch_shapes=scratch + [pltpu.VMEM((tiles * frames * around, LANES), jnp.float32)],
            compiler_params=params,
            name="front",
        )(*[kept(arg) for arg in args])
        arrived = lax.all_to_all(sent, ("ha", "wa"), split_axis=0, concat_axis=0, tiled=True)
        return arrived.reshape(tiles * frames, around, LANES)
    value = pl.pallas_call(
        functools.partial(front_kernel, rows, cols),
        out_shape=jax.ShapeDtypeStruct((count, LANES), jnp.bfloat16),
        in_specs=[anyw] * 5,
        out_specs=vmem,
        scratch_shapes=scratch,
        compiler_params=params,
        name="front",
    )(*[kept(arg) for arg in args])
    arrived = lax.all_to_all(
        value.reshape(each, tiles, LANES), ("ha", "wa"), split_axis=1, concat_axis=0, tiled=True
    )
    grid = arrived.reshape(count // (TH * TW), TH, TW, LANES)
    grid = padded_2(grid, (("ha", 1), ("wa", 2)), 1)
    return grid.reshape(grid.shape[0], around, LANES)


def feature_kernel(units_k, tok_ref, cw_any, cb_any, cols, flat, wide, feat, cw_ref, cb_ref, sems):
    copies = brought((cw_any, cb_any), (cw_ref, cb_ref), sems)
    place_ref = spots(units_k)
    has_up = place_ref[0] > 0
    has_down = place_ref[1] > 0
    has_left = place_ref[2] > 0
    has_right = place_ref[3] > 0
    rows_blk = TH + 1
    cols_blk = TW + 1
    frames, around, _ = tok_ref.shape
    c_lat = cw_ref.shape[1]
    c_in = cw_ref.shape[2]
    lanes = 4 * c_lat
    wide[...] = jnp.zeros_like(wide)
    for copy in copies:
        copy.wait()
    for p in range(2):
        for q in range(2):
            for r in range(3):
                for s in range(3):
                    tr, a = divmod(p + r, 2)
                    tc, e = divmod(q + s, 2)
                    base = (tr * 2 + tc) * lanes + (a * 2 + e) * c_lat
                    at = (p * 2 + q) * c_in
                    wide[base : base + c_lat, at : at + c_in] = cw_ref[r * 3 + s]
    for f in range(frames):
        flat[f * around : (f + 1) * around, :] = tok_ref[f].astype(jnp.float32)
    tok = [
        [flat[pl.ds(r * (TW + 2) + c, frames, stride=around), :] for c in range(TW + 2)] for r in range(TH + 2)
    ]
    block = []
    for m in range(rows_blk):
        for n in range(cols_blk):
            pairs = [
                tok[m + tr][n][:, :lanes] if lanes == LANES
                else tok[m + tr][n] + pltpu.roll(tok[m + tr][n + 1], lanes, 1)
                for tr in range(2)
            ]
            block.append(jnp.concatenate(pairs, axis=1))
    block = jnp.concatenate(block, axis=0).astype(jnp.bfloat16)
    for p in range(2):
        for q in range(2):
            at = (p * 2 + q) * c_in
            value = jnp.dot(block, wide[:, at : at + c_in], preferred_element_type=jnp.float32)
            value = silu(value + cb_ref[...]).astype(jnp.bfloat16).astype(jnp.float32)
            value = value.reshape(rows_blk, cols_blk, frames, c_in)
            for m in range(rows_blk):
                for n in range(cols_blk):
                    piece = value[m, n]
                    if m == 0 and p == 0:
                        piece = jnp.where(has_up, piece, 0.0)
                    if m == rows_blk - 1 and p == 1:
                        piece = jnp.where(has_down, piece, 0.0)
                    if n == 0 and q == 0:
                        piece = jnp.where(has_left, piece, 0.0)
                    if n == cols_blk - 1 and q == 1:
                        piece = jnp.where(has_right, piece, 0.0)
                    feat[2 * m + p, 2 * n + q] = piece
    height = 2 * rows_blk - 1
    breadth = 2 * cols_blk - 1
    rows_pad = cols.shape[0] // height
    filled = breadth * frames
    ck = c_in // units_k
    for k in range(units_k):
        at_k = pl.multiple_of(place_ref[6 + k] * ck, ck)
        for r in range(height):
            for rs in range(2):
                for cs in range(2):
                    value = feat[r + rs, cs : cs + breadth, :, pl.ds(at_k, ck)].reshape(filled, ck)
                    at = ((k * 2 + rs) * 2 + cs) * ck
                    cols[r * rows_pad : r * rows_pad + filled, at : at + ck] = value.astype(jnp.bfloat16)
    for r in range(height):
        if rows_pad > filled:
            cols[r * rows_pad + filled : (r + 1) * rows_pad, :] = jnp.zeros(
                (rows_pad - filled, cols.shape[1]), jnp.bfloat16
            )


def feature_call(tok, cw, cb, units_k):
    frames = tok.shape[0]
    c_in = cw.shape[2]
    rows_blk, cols_blk = TH + 1, TW + 1
    height, breadth = 2 * rows_blk - 1, 2 * cols_blk - 1
    rows_pad = -(-breadth * frames // 16) * 16
    vmem, anyw = VMEM, ANYWHERE
    return pl.pallas_call(
        functools.partial(feature_kernel, units_k),
        out_shape=jax.ShapeDtypeStruct((height * rows_pad, 4 * c_in), jnp.bfloat16),
        in_specs=[vmem, anyw, anyw],
        out_specs=vmem,
        scratch_shapes=[
            pltpu.VMEM((frames * tok.shape[1], LANES), jnp.float32),
            pltpu.VMEM((16 * C_LAT, 4 * c_in), jnp.bfloat16),
            pltpu.VMEM((2 * rows_blk, 2 * cols_blk, frames, c_in), jnp.float32),
            pltpu.VMEM(cw.shape, cw.dtype),
            pltpu.VMEM(cb.shape, cb.dtype),
            pltpu.SemaphoreType.DMA((2,)),
        ],
        compiler_params=pltpu.CompilerParams(vmem_limit_bytes=VMEM_BYTES),
        name="features",
    )(tok, kept(cw), kept(cb))


def fetch(units, place_ref, refs, held, sems):
    for u, unit in enumerate(units):
        for at, flags in unit:
            if flags is None:
                pltpu.make_async_copy(refs[at], held.at[u], sems.at[u]).start()
            else:
                hit = None
                for flag, want in flags:
                    now = place_ref[flag] == want
                    hit = now if hit is None else hit & now

                @pl.when(hit)
                def _(at=at, u=u):
                    pltpu.make_async_copy(refs[at], held.at[u], sems.at[u]).start()


def settle(units, refs, held, sems):
    for u, unit in enumerate(units):
        pltpu.make_async_copy(refs[unit[0][0]], held.at[u], sems.at[u]).wait()


def tap_sum(cols, held, first, a):
    units, _, _, ck, _ = held.shape
    stacked = jnp.concatenate(
        [
            jnp.concatenate([held[k, a + 2 * (1 - rs), 2 * (1 - cs) + b] for b in range(2)], axis=1)
            for k in range(units)
            for rs in range(2)
            for cs in range(2)
        ],
        axis=0,
    )
    part = cols[:, first * 4 * ck : (first + units) * 4 * ck]
    return jnp.dot(part, stacked, preferred_element_type=jnp.float32)


def settle_lines(total, bias, a, keeps, frames, even, odd):
    has_up, has_down, has_left, has_right = keeps
    height, breadth = 2 * TH + 1, 2 * TW + 1
    filled = breadth * frames
    rows_pad = total.shape[0] // height
    cn = total.shape[1] // 2
    pair = []
    for b in range(2):
        value = silu(total[:, b * cn : (b + 1) * cn] + bias)
        pair.append(value.reshape(height, rows_pad, cn)[:, :filled].reshape(height, breadth, frames, cn))
    for r in range(height):
        line = 2 * r + a
        v0, v1 = pair[0][r], pair[1][r]
        v0 = jnp.concatenate([jnp.where(has_left, v0[:1], 0.0), v0[1:]], axis=0)
        v1 = jnp.concatenate([v1[:-1], jnp.where(has_right, v1[-1:], 0.0)], axis=0)
        if line == 0:
            v0, v1 = jnp.where(has_up, v0, 0.0), jnp.where(has_up, v1, 0.0)
        if line == 2 * height - 1:
            v0, v1 = jnp.where(has_down, v0, 0.0), jnp.where(has_down, v1, 0.0)
        even[line] = jnp.stack([v0, v1], axis=1).reshape(2 * filled, cn).astype(jnp.bfloat16)
        odd[line] = jnp.stack([v1[:-1], v0[1:]], axis=1).reshape(2 * (filled - frames), cn).astype(jnp.bfloat16)


STEP = 2


def window_sum(even, odd, ow_ref, y, frames):
    span, depth = odd.shape[1], odd.shape[2]
    lhs = []
    for r in range(3):
        for s in range(3):
            if s == 1:
                value = odd[y + r : y + r + STEP]
            else:
                value = even[y + r : y + r + STEP, s * frames : s * frames + span]
            lhs.append(value.reshape(STEP * span, depth))
    rhs = ow_ref[...].reshape(9 * depth, ow_ref.shape[2])
    return jnp.dot(jnp.concatenate(lhs, axis=1), rhs, preferred_element_type=jnp.float32)


def early_kernel(plan, cols, *rest):
    count = len(rest) - 1 - 2 * len(plan)
    refs, sum_ref = rest[:count], rest[count]
    helds, sems = rest[count + 1 : count + 1 + len(plan)], rest[count + 1 + len(plan) :]
    place = spots(UNITS)
    for units, held, sem in zip(plan, helds, sems):
        fetch(units, place, refs, held, sem)
    for j, (units, held, sem) in enumerate(zip(plan, helds, sems)):
        settle(units, refs, held, sem)
        for a in range(2):
            sum_ref[j, a] = tap_sum(cols, held, 0, a)


def slice_kernel(units, first, total_units, slot, frames, ends, *rest):
    heads = 4 + (1 if ends else 0) + (0 if slot is None else 1)
    head, rest = list(rest[:heads]), rest[heads:]
    count = len(rest) - 7 - (1 if ends else 0)
    refs, rest = rest[:count], rest[count:]
    cols = head.pop(0)
    sum_ref = None if slot is None else head.pop(0)
    ub_ref, ow_any, ob_ref = head[:3]
    o_ref, rest = rest[0], rest[1:]
    if ends:
        part_ref, (tall, *rest) = head[3], rest
    even, odd, ow_ref, ow_sem, held, sems = rest
    place = spots(total_units)
    cn = held.shape[4]
    at = place[5] if not slot else 1 - place[5]
    at = pl.multiple_of(at * cn, cn)
    fetch(units, place, refs, held, sems)
    ow_copy = pltpu.make_async_copy(ow_any.at[:, pl.ds(at, cn), :], ow_ref, ow_sem)
    ow_copy.start()
    bias = ub_ref[:, pl.ds(at, cn)]
    keeps = tuple(place[i] > 0 for i in range(4))
    settle(units, refs, held, sems)
    for a in range(2):
        total = tap_sum(cols, held, first, a)
        if slot is not None:
            total = total + sum_ref[slot, a]
        settle_lines(total, bias, a, keeps, frames, even, odd)
    ow_copy.wait()
    span = odd.shape[1]
    for y in range(0, even.shape[0] - 2, STEP):
        total = window_sum(even, odd, ow_ref, y, frames)
        if not ends:
            o_ref[y * span : (y + STEP) * span, :] = total + ob_ref[...]
            continue
        store_rows(total + part_ref[y * span : (y + STEP) * span, :], y, tall, o_ref)


def store_rows(total, y, tall, o_ref):
    frames, _, out_w, _ = o_ref.shape
    part = tall.shape[2]
    for h in range(tall.shape[0]):
        tall[h] = total[:, h * part : (h + 1) * part]
        for d in range(STEP):
            for f in range(frames):
                line = tall[h, pl.ds(d * out_w * frames + f, out_w, stride=frames), :]
                o_ref[f, y + d, :, h * part : (h + 1) * part] = line.astype(jnp.bfloat16)


def order_kernel(part_ref, o_ref, tall):
    span = o_ref.shape[2] * o_ref.shape[0]
    for y in range(0, o_ref.shape[1], STEP):
        store_rows(part_ref[y * span : (y + STEP) * span, :], y, tall, o_ref)


def spots(units_k):
    rows, cols = lax.axis_size("ha"), lax.axis_size("wa")
    row, col, core = (lax.axis_index(axis) for axis in ("ha", "wa", "ta"))
    inside = [row > 0, row < rows - 1, col > 0, col < cols - 1]
    inside = [jnp.where(item, 1, 0) for item in inside]
    if units_k == 1:
        return inside + [core, 0, 0]
    beside = row + 1 - 2 * lax.rem(row, 2)
    order = [row, beside, rows - 1 - row, rows - 1 - beside]
    return inside + [core, col] + order + [inside[0] * inside[1]]


def work_space(frames, ow, shape, count):
    _, _, _, cn = shape
    height, breadth = 2 * TH + 1, 2 * TW + 1
    return [
        pltpu.VMEM((2 * height, 2 * breadth * frames, cn), jnp.bfloat16),
        pltpu.VMEM((2 * height, 2 * (breadth - 1) * frames, cn), jnp.bfloat16),
        pltpu.VMEM((ow.shape[0], cn, ow.shape[2]), ow.dtype),
        pltpu.SemaphoreType.DMA(()),
    ] + held_space(shape, count)


def held_space(shape, count):
    return [pltpu.VMEM((count,) + shape, jnp.bfloat16), pltpu.SemaphoreType.DMA((count,))]


def early_call(cols, plan, arrays):
    shape = arrays[0].shape
    spaces = [held_space(shape, len(units)) for units in plan]
    return pl.pallas_call(
        functools.partial(early_kernel, plan),
        out_shape=jax.ShapeDtypeStruct((len(plan), 2, cols.shape[0], 2 * shape[3]), jnp.float32),
        in_specs=[VMEM] + [ANYWHERE] * len(arrays),
        out_specs=VMEM,
        scratch_shapes=[space[0] for space in spaces] + [space[1] for space in spaces],
        compiler_params=pltpu.CompilerParams(vmem_limit_bytes=10 << 20),
        name="early",
    )(cols, *arrays)


def decoded_shape(frames, c_up):
    return (frames, 4 * TH, 4 * TW, c_up)


def slice_call(cols, sums, ub, ow, ob, part, units, first, total_units, slot, arrays, frames):
    c_up = ob.shape[1]
    ends = part is not None
    shape = decoded_shape(frames, c_up)
    args = (cols,) if sums is None else (cols, sums)
    args += (ub, kept(ow), ob)
    specs = [VMEM] * (len(args) - 2) + [ANYWHERE, VMEM]
    scratch = work_space(frames, ow, arrays[0].shape, len(units))
    out = jax.ShapeDtypeStruct((shape[0] * shape[1] * shape[2], c_up), jnp.float32)
    if ends:
        args += (part,)
        specs += [VMEM]
        scratch = [tall_space(shape)] + scratch
        out = jax.ShapeDtypeStruct(shape, jnp.bfloat16)
    return pl.pallas_call(
        functools.partial(slice_kernel, units, first, total_units, slot, frames, ends),
        out_shape=out,
        in_specs=specs + [ANYWHERE] * len(arrays),
        out_specs=VMEM,
        scratch_shapes=scratch,
        compiler_params=pltpu.CompilerParams(vmem_limit_bytes=14 << 20),
    )(*args, *arrays)


def tall_space(shape):
    return pltpu.VMEM((shape[3] // LANES, STEP * shape[2] * shape[0], LANES), jnp.float32)


def order_call(part, frames):
    shape = decoded_shape(frames, part.shape[1])
    return pl.pallas_call(
        order_kernel,
        out_shape=jax.ShapeDtypeStruct(shape, jnp.bfloat16),
        in_specs=[VMEM],
        out_specs=VMEM,
        scratch_shapes=[tall_space(shape)],
        compiler_params=pltpu.CompilerParams(vmem_limit_bytes=10 << 20),
        name="order",
    )(part)


def moves(rule, rows, cols, cores):
    pairs = []
    for h in range(rows):
        for w in range(cols):
            for t in range(cores):
                to = rule(h, w, t)
                if to is not None:
                    pairs.append((((h * cols) + w) * cores + t, ((to[0] * cols) + to[1]) * cores + to[2]))
    return pairs


def spread_kernel(weight):
    axes = ("ha", "wa", "ta")
    rows, cols, cores = (lax.axis_size(axis) for axis in axes)
    inner = lambda h: 0 < h < rows - 1

    def go(value, rule):
        return lax.ppermute(value, axes, moves(rule, rows, cols, cores))

    def across(value):
        return go(value, lambda h, w, t: (h, w, 1 - t))

    r1 = go(weight, lambda h, w, t: (h, 1 - w, 0) if t == 0 else (h ^ 1, w, 1))
    r2 = go(weight, lambda h, w, t: (rows - 1 - h, w, t) if inner(h) and t == 0 else None)
    r2x = go(weight, lambda h, w, t: (rows - 1 - h, w, t) if not inner(h) and t == 1 else None)
    r4 = go(r1, lambda h, w, t: (h, 1 - w, 1) if t == 1 else None)
    r3a = go(r1, lambda h, w, t: (rows - 1 - h, w, 1) if inner(h) and t == 1 else None)
    r3b = go(r2, lambda h, w, t: (h ^ 1, w, 0) if t == 0 else None)
    r5a = go(r2, lambda h, w, t: (h, 1 - w, t) if inner(h) and t == 0 else None)
    r5b = go(r2x, lambda h, w, t: (h, 1 - w, t) if not inner(h) and t == 1 else None)
    r6a = go(r3a, lambda h, w, t: (h, 1 - w, 1) if inner(h) and t == 1 else None)
    r6b = go(r3b, lambda h, w, t: (h, 1 - w, 0) if not inner(h) and t == 0 else None)
    c1, c2, c2x, c4 = across(r1), across(r2), across(r2x), across(r4)
    c3a, c3b, c5a, c5b = across(r3a), across(r3b), across(r5a), across(r5b)
    c6a, c6b = across(r6a), across(r6b)
    core, mid = 4, 6 + rows
    pick = lambda at, which, on: (at, ((mid, which), (core, on)))
    four = lambda a: [pick(a, 1, 0), pick(a + 1, 1, 1), pick(a + 2, 0, 1), pick(a + 3, 0, 0)]
    third = lambda a: [pick(a, 1, 1), pick(a + 1, 1, 0), pick(a + 2, 0, 0), pick(a + 3, 0, 1)]
    early = (
        ([(0, None)], [(1, ((core, 1),)), (2, ((core, 0),))], four(3)),
        ([(1, ((core, 0),)), (2, ((core, 1),))], [(7, ((core, 1),)), (8, ((core, 0),))]),
    )
    early_arrays = [weight, r1, c1, r2, c2, r2x, c2x, r4, c4]
    own, own_arrays = (third(0),), [r3a, c3a, r3b, c3b]
    late, late_arrays = (four(0), third(4)), [r5a, c5a, r5b, c5b, r6a, c6a, r6b, c6b]
    return early, early_arrays, own, own_arrays, late, late_arrays


def per_device(
    tokens,
    mod_scale,
    mod_shift,
    proj_weight,
    proj_bias,
    conv_weight,
    conv_bias,
    up_weight,
    up_bias,
    out_weight,
    out_bias,
):
    count_rows = lax.axis_size("ha")
    count_cols = lax.axis_size("wa")
    ck, cn = up_weight.shape[2], up_weight.shape[3]
    c_in, c_up = conv_weight.shape[3], out_weight.shape[3]
    split = (
        (count_rows, count_cols, lax.axis_size("ta")) == (UNITS, 2, 2) and ck % LANES == 0 and cn % LANES == 0
    )
    units_k = count_rows if split else 1
    local_tokens = tokens.reshape(tokens.shape[1], tokens.shape[2])
    if split:
        spread = spread_kernel(up_weight)
    else:
        whole = lax.all_gather(up_weight, "wa", axis=3, tiled=True)
        whole = lax.all_gather(whole, "ha", axis=2, tiled=True)
    tok = token_windows(
        local_tokens, mod_scale, mod_shift, proj_weight, proj_bias, count_rows, count_cols
    )
    frames = tok.shape[0]
    cols = feature_call(tok, conv_weight.reshape(9, C_LAT, c_in), conv_bias[None], units_k)
    ub, ob, ow = up_bias[None], out_bias[None], out_weight.reshape(9, c_up, c_up)
    if split:
        early, early_arrays, own, own_arrays, late, late_arrays = spread
        sums = early_call(cols, early, early_arrays)
        part = slice_call(cols, sums, ub, ow, ob, None, own, 3, UNITS, 0, own_arrays, frames)
        return slice_call(cols, sums, ub, ow, ob, part, late, 2, UNITS, 1, late_arrays, frames)
    part = slice_call(cols, None, ub, ow, ob, None, ([(0, None)],), 0, 1, None, [whole], frames)
    return order_call(part, frames)


def solution(mesh):
    placed = (
        P(("groups", "ta"), ("ha", "wa"), None),
        P("groups"),
        P("groups"),
        P(),
        P(),
        P(),
        P(),
        P(None, None, "ha", "wa"),
        P(),
        P(),
        P(),
    )
    return jax.shard_map(
        per_device,
        mesh=mesh,
        in_specs=placed,
        out_specs=P(("groups", "ta"), "ha", "wa", None),
        check_vma=False,
    )
```

```python
import functools

import jax
import jax.numpy as jnp
from jax import lax
from jax.experimental import pallas as pl
from jax.experimental.pallas import tpu as pltpu
from jax.sharding import PartitionSpec as P


C_LAT = 16
TH = 2
TW = 8
LANES = 128
VMEM_BYTES = 10 << 20
UNITS = 4
VMEM = pl.BlockSpec(memory_space=pltpu.VMEM)
ANYWHERE = pl.BlockSpec(memory_space=pl.ANY)


def silu(value):
    return value * jax.nn.sigmoid(value)


def padded_2(cells, sides, width):
    for axis, dim in sides:
        count = lax.axis_size(axis)
        ends = count - 1
        head = lax.slice_in_dim(cells, 0, width, axis=dim)
        tail = lax.slice_in_dim(cells, cells.shape[dim] - width, cells.shape[dim], axis=dim)
        cells = jnp.concatenate(
            [
                lax.ppermute(tail, axis, [(i, (i + 1) % count) for i in range(ends)]),
                cells,
                lax.ppermute(head, axis, [((i + 1) % count, i) for i in range(ends)]),
            ],
            axis=dim,
        )
    return cells


def kept(value):
    return pltpu.with_memory_space_constraint(value, pltpu.HBM)


def brought(sources, targets, sems):
    copies = [
        pltpu.make_async_copy(source, target, sems.at[i])
        for i, (source, target) in enumerate(zip(sources, targets))
    ]
    for copy in copies:
        copy.start()
    return copies


def front_kernel(rows, cols, *refs):
    sources, o_ref = refs[:5], refs[5]
    tok_ref, scale_ref, shift_ref, pw_ref, pb_ref, sems, patch = refs[6:13]
    copies = brought(sources, refs[6:11], sems)
    count, lanes = patch.shape
    width = pw_ref.shape[0]
    copies[0].wait()
    values = tok_ref[...].astype(jnp.float32)
    center = values - jnp.mean(values, axis=-1, keepdims=True)
    spread = jnp.mean(center * center, axis=-1, keepdims=True)
    for copy in copies[1:]:
        copy.wait()
    normed = center * lax.rsqrt(spread + 1e-06) * (1.0 + scale_ref[...]) + shift_ref[...]
    value = lax.dot_general(
        normed.astype(jnp.bfloat16),
        pw_ref[...],
        (((1,), (1,)), ((), ())),
        preferred_element_type=jnp.float32,
    )
    value = (value + pb_ref[...]).astype(jnp.bfloat16)
    source = lax.broadcasted_iota(jnp.int32, (width, lanes), 0)
    place = lax.broadcasted_iota(jnp.int32, (width, lanes), 1)
    chosen = source == (place % C_LAT) * (width // C_LAT) + place // C_LAT
    chosen = jnp.where(chosen & (place < width), 1.0, 0.0).astype(jnp.bfloat16)
    patch[...] = jnp.dot(value, chosen, preferred_element_type=jnp.float32)
    if len(refs) == 13:
        o_ref[...] = patch[...].astype(jnp.bfloat16)
        return
    window = refs[13]
    tiles = rows * cols
    frames = count // (tiles * TH * TW)
    window[...] = jnp.zeros_like(window)
    for h in range(rows):
        for w in range(cols):
            for f in range(frames):
                for d in range(TH + 2):
                    row = h * TH + d - 1
                    if not 0 <= row < rows * TH:
                        continue
                    base = (f * TH + row % TH) * TW * tiles + (row // TH) * cols
                    to = (((h * cols + w) * frames + f) * (TH + 2) + d) * (TW + 2)
                    window[to + 1 : to + 1 + TW, :] = patch[pl.ds(base + w, TW, stride=tiles), :]
                    if w > 0:
                        at = base + (TW - 1) * tiles + w - 1
                        window[to : to + 1, :] = patch[at : at + 1, :]
                    if w < cols - 1:
                        at = base + w + 1
                        window[to + 1 + TW : to + 2 + TW, :] = patch[at : at + 1, :]
    o_ref[...] = window[...].reshape(o_ref.shape).astype(jnp.bfloat16)


def token_windows(tokens, mod_scale, mod_shift, proj_weight, proj_bias, rows, cols):
    tiles = rows * cols
    count = tokens.shape[0]
    around = (TH + 2) * (TW + 2)
    vmem, anyw = VMEM, ANYWHERE
    args = (tokens, mod_scale[None], mod_shift[None], proj_weight.T, proj_bias[None])
    scratch = [pltpu.VMEM(arg.shape, arg.dtype) for arg in args]
    scratch += [pltpu.SemaphoreType.DMA((len(args),)), pltpu.VMEM((count, LANES), jnp.float32)]
    params = pltpu.CompilerParams(vmem_limit_bytes=VMEM_BYTES)
    each = count // tiles
    if each % (TH * TW) == 0:
        frames = each // (TH * TW)
        sent = pl.pallas_call(
            functools.partial(front_kernel, rows, cols),
            out_shape=jax.ShapeDtypeStruct((tiles, frames * around, LANES), jnp.bfloat16),
            in_specs=[anyw] * 5,
            out_specs=vmem,
            scratch_shapes=scratch + [pltpu.VMEM((tiles * frames * around, LANES), jnp.float32)],
            compiler_params=params,
            name="front",
        )(*[kept(arg) for arg in args])
        arrived = lax.all_to_all(sent, ("ha", "wa"), split_axis=0, concat_axis=0, tiled=True)
        return arrived.reshape(tiles * frames, around, LANES)
    value = pl.pallas_call(
        functools.partial(front_kernel, rows, cols),
        out_shape=jax.ShapeDtypeStruct((count, LANES), jnp.bfloat16),
        in_specs=[anyw] * 5,
        out_specs=vmem,
        scratch_shapes=scratch,
        compiler_params=params,
        name="front",
    )(*[kept(arg) for arg in args])
    arrived = lax.all_to_all(
        value.reshape(each, tiles, LANES), ("ha", "wa"), split_axis=1, concat_axis=0, tiled=True
    )
    grid = arrived.reshape(count // (TH * TW), TH, TW, LANES)
    grid = padded_2(grid, (("ha", 1), ("wa", 2)), 1)
    return grid.reshape(grid.shape[0], around, LANES)


def feature_kernel(units_k, tok_ref, cw_any, cb_any, cols, flat, wide, feat, cw_ref, cb_ref, sems):
    copies = brought((cw_any, cb_any), (cw_ref, cb_ref), sems)
    place_ref = spots(units_k)
    has_up = place_ref[0] > 0
    has_down = place_ref[1] > 0
    has_left = place_ref[2] > 0
    has_right = place_ref[3] > 0
    rows_blk = TH + 1
    cols_blk = TW + 1
    frames, around, _ = tok_ref.shape
    c_lat = cw_ref.shape[1]
    c_in = cw_ref.shape[2]
    lanes = 4 * c_lat
    wide[...] = jnp.zeros_like(wide)
    for copy in copies:
        copy.wait()
    for p in range(2):
        for q in range(2):
            for r in range(3):
                for s in range(3):
                    tr, a = divmod(p + r, 2)
                    tc, e = divmod(q + s, 2)
                    base = (tr * 2 + tc) * lanes + (a * 2 + e) * c_lat
                    at = (p * 2 + q) * c_in
                    wide[base : base + c_lat, at : at + c_in] = cw_ref[r * 3 + s]
    for f in range(frames):
        flat[f * around : (f + 1) * around, :] = tok_ref[f].astype(jnp.float32)
    tok = [
        [flat[pl.ds(r * (TW + 2) + c, frames, stride=around), :] for c in range(TW + 2)] for r in range(TH + 2)
    ]
    block = []
    for m in range(rows_blk):
        for n in range(cols_blk):
            pairs = [
                tok[m + tr][n][:, :lanes] if lanes == LANES
                else tok[m + tr][n] + pltpu.roll(tok[m + tr][n + 1], lanes, 1)
                for tr in range(2)
            ]
            block.append(jnp.concatenate(pairs, axis=1))
    block = jnp.concatenate(block, axis=0).astype(jnp.bfloat16)
    for p in range(2):
        for q in range(2):
            at = (p * 2 + q) * c_in
            value = jnp.dot(block, wide[:, at : at + c_in], preferred_element_type=jnp.float32)
            value = silu(value + cb_ref[...]).astype(jnp.bfloat16).astype(jnp.float32)
            value = value.reshape(rows_blk, cols_blk, frames, c_in)
            for m in range(rows_blk):
                for n in range(cols_blk):
                    piece = value[m, n]
                    if m == 0 and p == 0:
                        piece = jnp.where(has_up, piece, 0.0)
                    if m == rows_blk - 1 and p == 1:
                        piece = jnp.where(has_down, piece, 0.0)
                    if n == 0 and q == 0:
                        piece = jnp.where(has_left, piece, 0.0)
                    if n == cols_blk - 1 and q == 1:
                        piece = jnp.where(has_right, piece, 0.0)
                    feat[2 * m + p, 2 * n + q] = piece
    height = 2 * rows_blk - 1
    breadth = 2 * cols_blk - 1
    rows_pad = cols.shape[0] // height
    filled = breadth * frames
    ck = c_in // units_k
    for k in range(units_k):
        at_k = pl.multiple_of(place_ref[6 + k] * ck, ck)
        for r in range(height):
            for rs in range(2):
                for cs in range(2):
                    value = feat[r + rs, cs : cs + breadth, :, pl.ds(at_k, ck)].reshape(filled, ck)
                    at = ((k * 2 + rs) * 2 + cs) * ck
                    cols[r * rows_pad : r * rows_pad + filled, at : at + ck] = value.astype(jnp.bfloat16)
    for r in range(height):
        if rows_pad > filled:
            cols[r * rows_pad + filled : (r + 1) * rows_pad, :] = jnp.zeros(
                (rows_pad - filled, cols.shape[1]), jnp.bfloat16
            )


def feature_call(tok, cw, cb, units_k):
    frames = tok.shape[0]
    c_in = cw.shape[2]
    rows_blk, cols_blk = TH + 1, TW + 1
    height, breadth = 2 * rows_blk - 1, 2 * cols_blk - 1
    rows_pad = -(-breadth * frames // 16) * 16
    vmem, anyw = VMEM, ANYWHERE
    return pl.pallas_call(
        functools.partial(feature_kernel, units_k),
        out_shape=jax.ShapeDtypeStruct((height * rows_pad, 4 * c_in), jnp.bfloat16),
        in_specs=[vmem, anyw, anyw],
        out_specs=vmem,
        scratch_shapes=[
            pltpu.VMEM((frames * tok.shape[1], LANES), jnp.float32),
            pltpu.VMEM((16 * C_LAT, 4 * c_in), jnp.bfloat16),
            pltpu.VMEM((2 * rows_blk, 2 * cols_blk, frames, c_in), jnp.float32),
            pltpu.VMEM(cw.shape, cw.dtype),
            pltpu.VMEM(cb.shape, cb.dtype),
            pltpu.SemaphoreType.DMA((2,)),
        ],
        compiler_params=pltpu.CompilerParams(vmem_limit_bytes=VMEM_BYTES),
        name="features",
    )(tok, kept(cw), kept(cb))


def fetch(units, place_ref, refs, held, sems):
    for u, unit in enumerate(units):
        for at, flags in unit:
            if flags is None:
                pltpu.make_async_copy(refs[at], held.at[u], sems.at[u]).start()
            else:
                hit = None
                for flag, want in flags:
                    now = place_ref[flag] == want
                    hit = now if hit is None else hit & now

                @pl.when(hit)
                def _(at=at, u=u):
                    pltpu.make_async_copy(refs[at], held.at[u], sems.at[u]).start()


def settle(units, refs, held, sems):
    for u, unit in enumerate(units):
        pltpu.make_async_copy(refs[unit[0][0]], held.at[u], sems.at[u]).wait()


def tap_sum(cols, held, first, a):
    units, _, _, ck, _ = held.shape
    stacked = jnp.concatenate(
        [
            jnp.concatenate([held[k, a + 2 * (1 - rs), 2 * (1 - cs) + b] for b in range(2)], axis=1)
            for k in range(units)
            for rs in range(2)
            for cs in range(2)
        ],
        axis=0,
    )
    part = cols[:, first * 4 * ck : (first + units) * 4 * ck]
    return jnp.dot(part, stacked, preferred_element_type=jnp.float32)


def settle_lines(total, bias, a, keeps, frames, even, odd):
    has_up, has_down, has_left, has_right = keeps
    height, breadth = 2 * TH + 1, 2 * TW + 1
    filled = breadth * frames
    rows_pad = total.shape[0] // height
    cn = total.shape[1] // 2
    pair = []
    for b in range(2):
        value = silu(total[:, b * cn : (b + 1) * cn] + bias)
        pair.append(value.reshape(height, rows_pad, cn)[:, :filled].reshape(height, breadth, frames, cn))
    for r in range(height):
        line = 2 * r + a
        v0, v1 = pair[0][r], pair[1][r]
        v0 = jnp.concatenate([jnp.where(has_left, v0[:1], 0.0), v0[1:]], axis=0)
        v1 = jnp.concatenate([v1[:-1], jnp.where(has_right, v1[-1:], 0.0)], axis=0)
        if line == 0:
            v0, v1 = jnp.where(has_up, v0, 0.0), jnp.where(has_up, v1, 0.0)
        if line == 2 * height - 1:
            v0, v1 = jnp.where(has_down, v0, 0.0), jnp.where(has_down, v1, 0.0)
        even[line] = jnp.stack([v0, v1], axis=1).reshape(2 * filled, cn).astype(jnp.bfloat16)
        odd[line] = jnp.stack([v1[:-1], v0[1:]], axis=1).reshape(2 * (filled - frames), cn).astype(jnp.bfloat16)


STEP = 2


def window_sum(even, odd, ow_ref, y, frames):
    span, depth = odd.shape[1], odd.shape[2]
    lhs = []
    for r in range(3):
        for s in range(3):
            if s == 1:
                value = odd[y + r : y + r + STEP]
            else:
                value = even[y + r : y + r + STEP, s * frames : s * frames + span]
            lhs.append(value.reshape(STEP * span, depth))
    rhs = ow_ref[...].reshape(9 * depth, ow_ref.shape[2])
    return jnp.dot(jnp.concatenate(lhs, axis=1), rhs, preferred_element_type=jnp.float32)


def early_kernel(plan, first, slot, cols, *rest):
    before = None
    if slot is not None:
        before, rest = rest[0], rest[1:]
    count = len(rest) - 1 - 2 * len(plan)
    refs, sum_ref = rest[:count], rest[count]
    helds, sems = rest[count + 1 : count + 1 + len(plan)], rest[count + 1 + len(plan) :]
    place = spots(UNITS)
    for units, held, sem in zip(plan, helds, sems):
        fetch(units, place, refs, held, sem)
    for j, (units, held, sem) in enumerate(zip(plan, helds, sems)):
        settle(units, refs, held, sem)
        for a in range(2):
            total = tap_sum(cols, held, first, a)
            sum_ref[j, a] = total if before is None else total + before[slot + j, a]


def slice_kernel(units, first, total_units, slot, frames, ends, *rest):
    heads = 4 + (1 if ends else 0) + (0 if slot is None else 1)
    head, rest = list(rest[:heads]), rest[heads:]
    count = len(rest) - 7 - (1 if ends else 0)
    refs, rest = rest[:count], rest[count:]
    cols = head.pop(0)
    sum_ref = None if slot is None else head.pop(0)
    ub_ref, ow_any, ob_ref = head[:3]
    o_ref, rest = rest[0], rest[1:]
    if ends:
        part_ref, (tall, *rest) = head[3], rest
    even, odd, ow_ref, ow_sem, held, sems = rest
    place = spots(total_units)
    cn = held.shape[4]
    at = place[5] if not slot else 1 - place[5]
    at = pl.multiple_of(at * cn, cn)
    fetch(units, place, refs, held, sems)
    ow_copy = pltpu.make_async_copy(ow_any.at[:, pl.ds(at, cn), :], ow_ref, ow_sem)
    ow_copy.start()
    bias = ub_ref[:, pl.ds(at, cn)]
    keeps = tuple(place[i] > 0 for i in range(4))
    settle(units, refs, held, sems)
    for a in range(2):
        total = tap_sum(cols, held, first, a)
        if slot is not None:
            total = total + sum_ref[0, a]
        settle_lines(total, bias, a, keeps, frames, even, odd)
    ow_copy.wait()
    span = odd.shape[1]
    for y in range(0, even.shape[0] - 2, STEP):
        total = window_sum(even, odd, ow_ref, y, frames)
        if not ends:
            o_ref[y * span : (y + STEP) * span, :] = total + ob_ref[...]
            continue
        store_rows(total + part_ref[y * span : (y + STEP) * span, :], y, tall, o_ref)


def store_rows(total, y, tall, o_ref):
    frames, _, out_w, _ = o_ref.shape
    part = tall.shape[2]
    for h in range(tall.shape[0]):
        tall[h] = total[:, h * part : (h + 1) * part]
        for d in range(STEP):
            for f in range(frames):
                line = tall[h, pl.ds(d * out_w * frames + f, out_w, stride=frames), :]
                o_ref[f, y + d, :, h * part : (h + 1) * part] = line.astype(jnp.bfloat16)


def order_kernel(part_ref, o_ref, tall):
    span = o_ref.shape[2] * o_ref.shape[0]
    for y in range(0, o_ref.shape[1], STEP):
        store_rows(part_ref[y * span : (y + STEP) * span, :], y, tall, o_ref)


def spots(units_k):
    rows, cols = lax.axis_size("ha"), lax.axis_size("wa")
    row, col, core = (lax.axis_index(axis) for axis in ("ha", "wa", "ta"))
    inside = [row > 0, row < rows - 1, col > 0, col < cols - 1]
    inside = [jnp.where(item, 1, 0) for item in inside]
    if units_k == 1:
        return inside + [core, 0, 0]
    beside = row + 1 - 2 * lax.rem(row, 2)
    order = [row, beside, rows - 1 - row, rows - 1 - beside]
    return inside + [core, col] + order + [inside[0] * inside[1]]


def work_space(frames, ow, shape, count):
    _, _, _, cn = shape
    height, breadth = 2 * TH + 1, 2 * TW + 1
    return [
        pltpu.VMEM((2 * height, 2 * breadth * frames, cn), jnp.bfloat16),
        pltpu.VMEM((2 * height, 2 * (breadth - 1) * frames, cn), jnp.bfloat16),
        pltpu.VMEM((ow.shape[0], cn, ow.shape[2]), ow.dtype),
        pltpu.SemaphoreType.DMA(()),
    ] + held_space(shape, count)


def held_space(shape, count):
    return [pltpu.VMEM((count,) + shape, jnp.bfloat16), pltpu.SemaphoreType.DMA((count,))]


def early_call(cols, plan, first, sums, slot, arrays):
    shape = arrays[0].shape
    spaces = [held_space(shape, len(units)) for units in plan]
    args = (cols,) if sums is None else (cols, sums)
    return pl.pallas_call(
        functools.partial(early_kernel, plan, first, slot),
        out_shape=jax.ShapeDtypeStruct((len(plan), 2, cols.shape[0], 2 * shape[3]), jnp.float32),
        in_specs=[VMEM] * len(args) + [ANYWHERE] * len(arrays),
        out_specs=VMEM,
        scratch_shapes=[space[0] for space in spaces] + [space[1] for space in spaces],
        compiler_params=pltpu.CompilerParams(vmem_limit_bytes=10 << 20),
    )(*args, *arrays)


def decoded_shape(frames, c_up):
    return (frames, 4 * TH, 4 * TW, c_up)


def slice_call(cols, sums, ub, ow, ob, part, units, first, total_units, slot, arrays, frames):
    c_up = ob.shape[1]
    ends = part is not None
    shape = decoded_shape(frames, c_up)
    args = (cols,) if sums is None else (cols, sums)
    args += (ub, kept(ow), ob)
    specs = [VMEM] * (len(args) - 2) + [ANYWHERE, VMEM]
    scratch = work_space(frames, ow, arrays[0].shape, len(units))
    out = jax.ShapeDtypeStruct((shape[0] * shape[1] * shape[2], c_up), jnp.float32)
    if ends:
        args += (part,)
        specs += [VMEM]
        scratch = [tall_space(shape)] + scratch
        out = jax.ShapeDtypeStruct(shape, jnp.bfloat16)
    outs = [out]
    return pl.pallas_call(
        functools.partial(slice_kernel, units, first, total_units, slot, frames, ends),
        out_shape=outs,
        in_specs=specs + [ANYWHERE] * len(arrays),
        out_specs=[VMEM] * len(outs),
        scratch_shapes=scratch,
        compiler_params=pltpu.CompilerParams(vmem_limit_bytes=15 << 20),
    )(*args, *arrays)


def tall_space(shape):
    return pltpu.VMEM((shape[3] // LANES, STEP * shape[2] * shape[0], LANES), jnp.float32)


def order_call(part, frames):
    shape = decoded_shape(frames, part.shape[1])
    return pl.pallas_call(
        order_kernel,
        out_shape=jax.ShapeDtypeStruct(shape, jnp.bfloat16),
        in_specs=[VMEM],
        out_specs=VMEM,
        scratch_shapes=[tall_space(shape)],
        compiler_params=pltpu.CompilerParams(vmem_limit_bytes=10 << 20),
        name="order",
    )(part)


def moves(rule, rows, cols, cores):
    pairs = []
    for h in range(rows):
        for w in range(cols):
            for t in range(cores):
                to = rule(h, w, t)
                if to is not None:
                    pairs.append((((h * cols) + w) * cores + t, ((to[0] * cols) + to[1]) * cores + to[2]))
    return pairs


def spread_kernel(weight):
    axes = ("ha", "wa", "ta")
    rows, cols, cores = (lax.axis_size(axis) for axis in axes)
    inner = lambda h: 0 < h < rows - 1

    def go(value, rule):
        return lax.ppermute(value, axes, moves(rule, rows, cols, cores))

    def across(value):
        return go(value, lambda h, w, t: (h, w, 1 - t))

    last = rows - 1

    nothing = lambda h, w: None

    def each(*rules):
        return lambda h, w, t: rules[t if inner(h) else 2 + t](h, w)

    r1 = go(
        weight,
        each(
            lambda h, w: (last - h, w, 0),
            lambda h, w: (h ^ 1, w, 1),
            lambda h, w: (h, 1 - w, 0),
            lambda h, w: (h ^ 1, w, 1),
        ),
    )
    r2 = go(weight, each(lambda h, w: (h, 1 - w, 0), nothing, nothing, lambda h, w: (last - h, w, 1)))
    r3 = go(
        r1,
        each(
            lambda h, w: (h ^ 1, w, 1),
            lambda h, w: (last - h, w, 1),
            lambda h, w: (h ^ 1, w, 0),
            lambda h, w: (h, w, 0),
        ),
    )
    r4 = go(
        r1,
        each(
            lambda h, w: (h, 1 - w, 1),
            lambda h, w: (h, w, 0),
            lambda h, w: (h, w, 1),
            lambda h, w: (h, 1 - w, 0),
        ),
    )
    r5 = go(
        r2,
        each(
            lambda h, w: (h, w, 1),
            lambda h, w: (h, w, 0),
            lambda h, w: (h, w, 1),
            lambda h, w: (h, 1 - w, 0),
        ),
    )
    r6 = go(
        r3,
        each(
            lambda h, w: (h, w, 1),
            lambda h, w: (h, 1 - w, 0),
            lambda h, w: (h, w, 1),
            lambda h, w: (h, 1 - w, 0),
        ),
    )
    mine = (r1, r2, r3, r4, r5, r6)
    theirs = [across(value) for value in mine]
    core, mid = 4, 6 + rows

    def unit(arrays, *places):
        choice = []
        for inside, which, on in places:
            for found, side in ((mine, on), (theirs, 1 - on)):
                at = next(i for i, array in enumerate(arrays) if array is found[which - 1])
                choice.append((at, ((mid, inside), (core, side))))
        return choice

    def both(*numbers):
        return [side[number - 1] for number in numbers for side in (mine, theirs)]

    early_arrays = [weight] + both(1, 2)
    early = (
        ([(0, None)], unit(early_arrays, (1, 1, 1), (0, 1, 1))),
        (unit(early_arrays, (1, 2, 0), (0, 1, 0)),),
    )
    own_arrays = both(1, 2, 3)
    own = (unit(own_arrays, (1, 1, 0), (0, 2, 1)), unit(own_arrays, (1, 3, 1), (0, 3, 1)))
    extra_arrays = both(3, 4, 5)
    extra = ((unit(extra_arrays, (1, 3, 0), (0, 4, 0)), unit(extra_arrays, (1, 4, 1), (0, 5, 0))),)
    late_arrays = both(6)
    late = (unit(late_arrays, (1, 6, 0), (0, 6, 0)),)
    return early, early_arrays, own, own_arrays, extra, extra_arrays, late, late_arrays


def per_device(
    tokens,
    mod_scale,
    mod_shift,
    proj_weight,
    proj_bias,
    conv_weight,
    conv_bias,
    up_weight,
    up_bias,
    out_weight,
    out_bias,
):
    count_rows = lax.axis_size("ha")
    count_cols = lax.axis_size("wa")
    ck, cn = up_weight.shape[2], up_weight.shape[3]
    c_in, c_up = conv_weight.shape[3], out_weight.shape[3]
    split = (
        (count_rows, count_cols, lax.axis_size("ta")) == (UNITS, 2, 2) and ck % LANES == 0 and cn % LANES == 0
    )
    units_k = count_rows if split else 1
    local_tokens = tokens.reshape(tokens.shape[1], tokens.shape[2])
    if split:
        spread = spread_kernel(up_weight)
    else:
        whole = lax.all_gather(up_weight, "wa", axis=3, tiled=True)
        whole = lax.all_gather(whole, "ha", axis=2, tiled=True)
    tok = token_windows(
        local_tokens, mod_scale, mod_shift, proj_weight, proj_bias, count_rows, count_cols
    )
    frames = tok.shape[0]
    cols = feature_call(tok, conv_weight.reshape(9, C_LAT, c_in), conv_bias[None], units_k)
    ub, ob, ow = up_bias[None], out_bias[None], out_weight.reshape(9, c_up, c_up)
    if split:
        early, early_arrays, own, own_arrays, extra, extra_arrays, late, late_arrays = spread
        sums = early_call(cols, early, 0, None, None, early_arrays)
        (part,) = slice_call(cols, sums, ub, ow, ob, None, own, 2, UNITS, 0, own_arrays, frames)
        more = early_call(cols, extra, 1, sums, 1, extra_arrays)
        return slice_call(cols, more, ub, ow, ob, part, late, 3, UNITS, 1, late_arrays, frames)[0]
    units = ([(0, None)],)
    (part,) = slice_call(cols, None, ub, ow, ob, None, units, 0, 1, None, [whole], frames)
    return order_call(part, frames)


def solution(mesh):
    placed = (
        P(("groups", "ta"), ("ha", "wa"), None),
        P("groups"),
        P("groups"),
        P(),
        P(),
        P(),
        P(),
        P(None, None, "ha", "wa"),
        P(),
        P(),
        P(),
    )
    return jax.shard_map(
        per_device,
        mesh=mesh,
        in_specs=placed,
        out_specs=P(("groups", "ta"), "ha", "wa", None),
        check_vma=False,
    )
```
